256 devices in a mesh: tm: 64 (over y_lo, x, z), freq: 4 (over y_hi, core).
Axes of the slice: x: 4, y: 4 (y_hi: 2, y_lo: 2; y = y_hi * 2 + y_lo), z: 8, core: 2. Of those that a mesh axis runs over, the one named last changes fastest.
Arguments:
- visibilities: bfloat16 [2, 32, 2048, 4096], P(None, 'freq', 'tm'), may hold values from -6 to 6
- feed_gains: float32 [2, 32, 1024], P(None, 'freq'), may hold values from -4 to 4
- feed_pairs: int32 [4096, 2], replicated, may hold values from 0 to 1023
- m_order: int32 [64], replicated, may hold values from 0 to 63, each once
- beam_rows: bfloat16 [2, 64, 32, 64, 4096], P(None, 'tm', 'freq'), may hold values from -0.0625 to 0.0625
- kl_basis: bfloat16 [64, 32, 64, 512], P('tm', 'freq'), may hold values from -0.125 to 0.125
Outputs:
- kl_modes: float32 [2, 64, 512], P(None, 'tm', 'freq')
The draws below stay inside these ranges and needn't reach their ends.
Inputs may be any that keep to these rules, and one draw needn't show every extreme that they name: `m_order`: each value appears once.
All inputs are finite; a program needn't handle non-finite values.
Results may differ from the reference program's by a relative error of at most 0.0057.
Values may be sent and summed in bfloat16 or wider, within the bound.
A program may use at most 128 MiB of HBM per device.

```python
import jax
import jax.numpy as jnp
from jax import lax

F = 32
T_SIZE = 2048
B = 4096
NFEED = 1024
K = 64
E = 512
M = 64


def touch_ends(entries, rng, smallest, largest):
    longest = entries.shape.index(max(entries.shape))
    spots = []
    for shift in (0, 1):
        where = [jax.random.randint(jax.random.fold_in(rng, axis), (), 0, length) for axis, length in enumerate(entries.shape)]
        where[longest] = (where[longest] + shift) % entries.shape[longest]
        spots.append(tuple(where))
    return entries.at[spots[0]].set(smallest).at[spots[1]].set(largest)


def levels(own_key, dims, cuts, smallest, top_value):
    gain = 1.0
    for position, shards_of in cuts:
        steps = jax.random.uniform(jax.random.fold_in(jax.random.fold_in(own_key, 6), position), (shards_of,), jnp.float32, smallest / len(cuts), top_value / len(cuts))
        gain = gain * jnp.repeat(jnp.exp(steps), dims[position] // shards_of).reshape((-1,) + (1,) * (len(dims) - 1 - position))
    return gain


def scatter_about(key, dims, scale, limit, pieces=(), kind=jnp.bfloat16):
    level = levels(key, dims, pieces, -0.22, 0.18) if pieces else 1.0
    entries = jax.random.normal(key, dims, jnp.float32) * scale * level
    return jnp.minimum(jnp.maximum(entries, -limit), limit).astype(kind)


def setup_inputs(seed: int = 0) -> dict:
    keys = jax.random.split(jax.random.key(seed), 7)
    visibilities = scatter_about(keys[0], (2, F, T_SIZE, B), 1.0, 6.0, ((1, 4), (2, 64)))
    feed_gains = scatter_about(keys[1], (2, F, NFEED), 0.8, 4.0, ((1, 4),), jnp.float32)
    feed_pairs = touch_ends(jax.random.randint(keys[2], (B, 2), 0, NFEED), jax.random.fold_in(keys[2], 1), 0, NFEED - 1).astype(jnp.int32)
    m_order = jax.random.permutation(keys[3], M).astype(jnp.int32)
    beam_rows = scatter_about(keys[4], (2, M, F, K, B), (2 * B) ** -0.5, 0.0625, ((1, 64), (2, 4)))
    kl_basis = scatter_about(keys[5], (M, F, K, E), (F * K) ** -0.5, 0.125, ((0, 64), (1, 4)))
    return dict(visibilities=visibilities, feed_gains=feed_gains, feed_pairs=feed_pairs, m_order=m_order, beam_rows=beam_rows, kl_basis=kl_basis)


def twiddle_table(m_order):
    shifted = (m_order - M // 2).astype(jnp.int32)
    times = jnp.arange(T_SIZE, dtype=jnp.int32)
    phase = shifted[:, None] * times[None, :] % T_SIZE
    angle = 2.0 * jnp.pi / T_SIZE * phase.astype(jnp.float32)
    norm = 1.0 / jnp.sqrt(jnp.float32(T_SIZE))
    cosine = jnp.cos(angle) * norm
    sine = jnp.sin(angle) * norm
    table = jnp.stack([jnp.stack([cosine, sine]), jnp.stack([-sine, cosine])])
    return table.astype(jnp.bfloat16)

def reference(visibilities, feed_gains, feed_pairs, m_order, beam_rows, kl_basis):
    table = twiddle_table(m_order).astype(jnp.float32)
    first = feed_pairs[:, 0]
    second = feed_pairs[:, 1]

    def one_channel(index):
        gains = feed_gains[:, index, :]
        gain_i = jnp.take(gains, first, axis=1)
        gain_j = jnp.take(gains, second, axis=1)
        prod_re = gain_i[0] * gain_j[0] + gain_i[1] * gain_j[1]
        prod_im = gain_i[1] * gain_j[0] - gain_i[0] * gain_j[1]
        raw = visibilities[:, index].astype(jnp.float32)
        cal_re = raw[0] * prod_re - raw[1] * prod_im
        cal_im = raw[0] * prod_im + raw[1] * prod_re
        calibrated = jnp.stack([cal_re, cal_im]).astype(jnp.bfloat16).astype(jnp.float32)
        spectrum = jnp.einsum('oimt,itb->omb', table, calibrated).astype(jnp.bfloat16).astype(jnp.float32)
        beam = beam_rows[:, :, index].astype(jnp.float32)
        tel_re = jnp.einsum('mkb,mb->mk', beam[0], spectrum[0]) - jnp.einsum('mkb,mb->mk', beam[1], spectrum[1])
        tel_im = jnp.einsum('mkb,mb->mk', beam[0], spectrum[1]) + jnp.einsum('mkb,mb->mk', beam[1], spectrum[0])
        return jnp.stack([tel_re, tel_im]).astype(jnp.bfloat16)
    telescope = lax.map(one_channel, jnp.arange(F, dtype=jnp.int32))
    telescope = telescope.astype(jnp.float32)
    basis = kl_basis.astype(jnp.float32)
    return jnp.einsum('fcmk,mfke->cme', telescope, basis)
```

```python
import functools

import jax
import jax.numpy as jnp
from jax import lax
from jax.experimental import pallas as pl
from jax.experimental.pallas import tpu as pltpu
from jax.sharding import PartitionSpec as P

DEPTH = 3


def kernel(
    dims,
    vis,
    gains,
    pairs,
    order,
    beam,
    basis,
    out,
    x_buf,
    part,
    gathered,
    rows32,
    spec_out,
    spec_in,
    beam_v,
    basis_v,
    gains_v,
    pairs_v,
    order_v,
    table_v,
    prod_v,
    share_out,
    share_in,
    raw_send,
    raw_recv,
    raw_own,
    part_send,
    part_recv,
    part_own,
    spec_send,
    spec_recv,
    spec_own,
    share_send,
    share_recv,
    load_sem,
):
    groups_j, groups_z, parts_f, chans, times, block, kept = dims
    slots = groups_j * groups_z
    length = slots * times
    tm = lax.axis_index("tm")
    fq = lax.axis_index("freq")
    me_j = tm // groups_z
    me_z = tm % groups_z

    def dev_j(o):
        return (lax.rem(me_j + o, groups_j) * groups_z + me_z, fq)

    def dev_z(o):
        return (me_j * groups_z + lax.rem(me_z + o, groups_z), fq)

    def dev_f(o):
        return (tm, lax.rem(fq + o, parts_f))

    barrier = pltpu.get_barrier_semaphore()
    peers = (
        [dev_j(o) for o in range(1, groups_j)]
        + [dev_z(o) for o in range(1, groups_z)]
        + [dev_f(o) for o in range(1, parts_f)]
    )
    for peer in peers:
        pl.semaphore_signal(barrier, inc=1, device_id=peer, device_id_type=pl.DeviceIdType.MESH)
    pl.semaphore_wait(barrier, len(peers))

    def raw_copy(f, o):
        to = lax.rem(me_j + o, groups_j)
        return pltpu.make_async_remote_copy(
            src_ref=vis.at[:, f, :, pl.ds(pl.multiple_of(to * block, block), block)],
            dst_ref=x_buf.at[f, :, pl.ds(pl.multiple_of(me_j * times, times), times), :],
            send_sem=raw_send.at[f, o],
            recv_sem=raw_recv.at[f, o],
            device_id=dev_j(o),
            device_id_type=pl.DeviceIdType.MESH,
        )

    def own_copy(f):
        return pltpu.make_async_copy(
            vis.at[:, f, :, pl.ds(pl.multiple_of(me_j * block, block), block)],
            x_buf.at[f, :, pl.ds(pl.multiple_of(me_j * times, times), times), :],
            raw_own.at[f],
        )

    def start_raw(f):
        for o in range(1, groups_j):
            raw_copy(f, o).start()
        own_copy(f).start()

    loads = [
        pltpu.make_async_copy(order, order_v, load_sem.at[0]),
        pltpu.make_async_copy(pairs, pairs_v, load_sem.at[1]),
        pltpu.make_async_copy(gains, gains_v, load_sem.at[2]),
    ]
    late_loads = [pltpu.make_async_copy(basis, basis_v, load_sem.at[3])] + [
        pltpu.make_async_copy(beam.at[:, :, i * block : (i + 1) * block], beam_v.at[i], load_sem.at[4 + i])
        for i in range(groups_j)
    ]
    for copy in loads:
        copy.start()
    for f in range(DEPTH):
        start_raw(f)
    for copy in late_loads:
        copy.start()
    for copy in loads:
        copy.wait()

    n_rows = 2 * slots
    n_cols = 2 * groups_j * times
    row_s = lax.broadcasted_iota(jnp.int32, (n_rows, slots), 0)
    slot_of_row = row_s % groups_j * groups_z + row_s // (2 * groups_j)
    chosen = lax.broadcasted_iota(jnp.int32, (n_rows, slots), 1) == slot_of_row
    mode = jnp.sum(jnp.where(chosen, order_v[...].astype(jnp.float32), 0.0), axis=1, keepdims=True)
    shifted = mode.astype(jnp.int32) - slots // 2
    row = lax.broadcasted_iota(jnp.int32, (n_rows, n_cols), 0)
    col = lax.broadcasted_iota(jnp.int32, (n_rows, n_cols), 1)
    part_out = row // groups_j % 2
    part_in = col // (groups_j * times)
    local = col % (groups_j * times)
    time = (local // times * groups_z + me_z) * times + local % times
    quarter = (part_out - part_in) * (length // 4)
    phase = (shifted * time + quarter) & (length - 1)
    angle = 2.0 * jnp.pi / length * phase.astype(jnp.float32)
    norm = 1.0 / jnp.sqrt(jnp.float32(length))
    table_v[...] = (jnp.cos(angle) * norm).astype(jnp.bfloat16)

    whole = gains_v[...]
    high = whole.astype(jnp.bfloat16)
    rest = whole - high.astype(jnp.float32)
    middle = rest.astype(jnp.bfloat16)
    low = (rest - middle.astype(jnp.float32)).astype(jnp.bfloat16)
    terms = jnp.concatenate([high, middle, low], axis=0)
    feeds = lax.broadcasted_iota(jnp.int32, (whole.shape[1], block), 0)
    columns = pl.ds(pl.multiple_of(me_j * block, block), block)
    picked = []
    for side in range(2):
        picker = (feeds == pairs_v[side : side + 1, columns]).astype(jnp.float32).astype(jnp.bfloat16)
        found = jnp.dot(terms, picker, preferred_element_type=jnp.float32)
        n = 2 * chans
        picked.append(found[:n] + found[n : 2 * n] + found[2 * n :])
    gi_re, gi_im = picked[0][:chans], picked[0][chans:]
    gj_re, gj_im = picked[1][:chans], picked[1][chans:]
    prod_v[0] = gi_re * gj_re + gi_im * gj_im
    prod_v[1] = gi_im * gj_re - gi_re * gj_im

    def part_copy(f, o):
        to = lax.rem(me_z + o, groups_z)
        return pltpu.make_async_remote_copy(
            src_ref=part.at[f, to],
            dst_ref=gathered.at[f, me_z],
            send_sem=part_send.at[f, o],
            recv_sem=part_recv.at[f, o],
            device_id=dev_z(o),
            device_id_type=pl.DeviceIdType.MESH,
        )

    def part_own_copy(f):
        return pltpu.make_async_copy(part.at[f, me_z], gathered.at[f, me_z], part_own.at[f])

    def transform(f):
        own_copy(f).wait()
        for o in range(1, groups_j):
            raw_copy(f, o).wait_recv()
        data = x_buf[f].reshape(n_cols, block)
        sums = jnp.dot(table_v[...], data, preferred_element_type=jnp.float32)
        part[f] = sums.astype(jnp.bfloat16).reshape(groups_z, 2 * groups_j, block)
        for o in range(1, groups_z):
            part_copy(f, o).start()
        part_own_copy(f).start()

    def combine(f):
        part_own_copy(f).wait()
        for o in range(1, groups_z):
            part_copy(f, o).wait_recv()
        total = gathered[f, 0].astype(jnp.float32)
        for i in range(1, groups_z):
            total = total + gathered[f, i].astype(jnp.float32)
        p_re = prod_v[0, pl.ds(f, 1), :]
        p_im = prod_v[1, pl.ds(f, 1), :]
        t_re, t_im = total[:groups_j], total[groups_j:]
        s_re = t_re * p_re - t_im * p_im
        s_im = t_re * p_im + t_im * p_re
        for i in range(groups_j):
            rows32[i, pl.ds(f, 1), :] = s_re[i : i + 1]
            rows32[i, pl.ds(chans + f, 1), :] = s_im[i : i + 1]

    def step(f, carry):
        @pl.when(f + DEPTH < chans)
        def _():
            start_raw(f + DEPTH)

        transform(f)

        @pl.when(f >= 1)
        def _():
            combine(f - 1)

        return carry

    lax.fori_loop(0, chans, step, 0)
    combine(chans - 1)

    def spec_copy(o):
        to = lax.rem(me_j + o, groups_j)
        return pltpu.make_async_remote_copy(
            src_ref=spec_out.at[to],
            dst_ref=spec_in.at[me_j],
            send_sem=spec_send.at[o],
            recv_sem=spec_recv.at[o],
            device_id=dev_j(o),
            device_id_type=pl.DeviceIdType.MESH,
        )

    spec_out[...] = rows32[...].astype(jnp.bfloat16)
    for o in range(1, groups_j):
        spec_copy(o).start()
    own_spec = pltpu.make_async_copy(spec_out.at[me_j], spec_in.at[me_j], spec_own)
    own_spec.start()
    for copy in late_loads:
        copy.wait()
    own_spec.wait()
    for o in range(1, groups_j):
        spec_copy(o).wait_recv()

    contract = (((1,), (1,)), ((), ()))
    tel = jnp.zeros((chans * kept, 2 * chans), jnp.float32)
    for i in range(groups_j):
        spec = spec_in[i]
        wide = spec.astype(jnp.float32)
        turned = jnp.concatenate([-wide[chans:], wide[:chans]], axis=0).astype(jnp.bfloat16)
        tel = tel + lax.dot_general(beam_v[i, 0], spec, contract, preferred_element_type=jnp.float32)
        tel = tel + lax.dot_general(beam_v[i, 1], turned, contract, preferred_element_type=jnp.float32)
    chan_row = lax.broadcasted_iota(jnp.int32, tel.shape, 0) // kept
    chan_col = lax.broadcasted_iota(jnp.int32, tel.shape, 1) % chans
    tel = jnp.where(chan_row == chan_col, tel, 0.0).astype(jnp.bfloat16)
    modes = lax.dot_general(tel, basis_v[...], (((0,), (0,)), ((), ())), preferred_element_type=jnp.float32)
    shares = jnp.sum(modes.reshape(2, chans, modes.shape[1]), axis=1)
    width = modes.shape[1] // parts_f
    share_out[...] = jnp.zeros(share_out.shape, jnp.float32)
    for i in range(parts_f):
        share_out[i, 0:2, :] = shares[:, i * width : (i + 1) * width]

    def share_copy(o):
        to = lax.rem(fq + o, parts_f)
        return pltpu.make_async_remote_copy(
            src_ref=share_out.at[to],
            dst_ref=share_in.at[o],
            send_sem=share_send.at[o],
            recv_sem=share_recv.at[o],
            device_id=dev_f(o),
            device_id_type=pl.DeviceIdType.MESH,
        )

    for o in range(1, parts_f):
        share_copy(o).start()
    total = share_out[fq]
    for o in range(1, parts_f):
        share_copy(o).wait_recv()
        total = total + share_in[o]
    out[...] = total[0:2]

    def drain(f, carry):
        for o in range(1, groups_j):
            raw_copy(f, o).wait_send()
        for o in range(1, groups_z):
            part_copy(f, o).wait_send()
        return carry

    lax.fori_loop(0, chans, drain, 0)
    for o in range(1, groups_j):
        spec_copy(o).wait_send()
    for o in range(1, parts_f):
        share_copy(o).wait_send()


def on_device(groups_j, visibilities, feed_gains, feed_pairs, m_order, beam_rows, kl_basis):
    groups_z = lax.axis_size("tm") // groups_j
    parts_f = lax.axis_size("freq")
    chans, times, baselines = visibilities.shape[1:]
    kept = beam_rows.shape[3]
    modes = kl_basis.shape[3]
    block = baselines // groups_j
    slots = groups_j * groups_z
    dims = (groups_j, groups_z, parts_f, chans, times, block, kept)
    feeds = feed_gains.shape[2]
    width = modes // parts_f
    bf16, f32 = jnp.bfloat16, jnp.float32
    dma = pltpu.SemaphoreType.DMA
    result = pl.pallas_call(
        functools.partial(kernel, dims),
        out_shape=jax.ShapeDtypeStruct((2, width), f32),
        in_specs=[pl.BlockSpec(memory_space=pltpu.HBM)] * 6,
        out_specs=pl.BlockSpec(memory_space=pltpu.VMEM),
        scratch_shapes=[
            pltpu.VMEM((chans, 2, groups_j * times, block), bf16),
            pltpu.VMEM((chans, groups_z, 2 * groups_j, block), bf16),
            pltpu.VMEM((chans, groups_z, 2 * groups_j, block), bf16),
            pltpu.VMEM((groups_j, 2 * chans, block), f32),
            pltpu.VMEM((groups_j, 2 * chans, block), bf16),
            pltpu.VMEM((groups_j, 2 * chans, block), bf16),
            pltpu.VMEM((groups_j, 2, chans * kept, block), bf16),
            pltpu.VMEM((chans * kept, modes), bf16),
            pltpu.VMEM((2 * chans, feeds), f32),
            pltpu.VMEM((2, baselines), jnp.int32),
            pltpu.VMEM((1, slots), jnp.int32),
            pltpu.VMEM((2 * slots, 2 * groups_j * times), bf16),
            pltpu.VMEM((2, chans, block), f32),
            pltpu.VMEM((parts_f, 8, width), f32),
            pltpu.VMEM((parts_f, 8, width), f32),
            dma((chans, groups_j)),
            dma((chans, groups_j)),
            dma((chans,)),
            dma((chans, groups_z)),
            dma((chans, groups_z)),
            dma((chans,)),
            dma((groups_j,)),
            dma((groups_j,)),
            dma,
            dma((parts_f,)),
            dma((parts_f,)),
            dma((4 + groups_j,)),
        ],
        compiler_params=pltpu.CompilerParams(
            collective_id=0, has_side_effects=True, vmem_limit_bytes=48 * 2**20
        ),
    )(
        visibilities,
        feed_gains.reshape(2 * chans, feeds),
        feed_pairs.T,
        m_order.reshape(1, slots),
        beam_rows.reshape(2, chans * kept, baselines),
        kl_basis.reshape(chans * kept, modes),
    )
    return result.reshape(2, 1, width)


def solution(mesh, groups_j=8):
    placed = (
        P(None, "freq", "tm", None),
        P(None, "freq", None),
        P(),
        P(),
        P(None, "tm", "freq", None, None),
        P("tm", "freq", None, None),
    )
    return jax.shard_map(
        functools.partial(on_device, groups_j),
        mesh=mesh,
        in_specs=placed,
        out_specs=P(None, "tm", "freq"),
        check_vma=False,
    )
```

```python
import functools
from types import SimpleNamespace

import jax
import jax.numpy as jnp
from jax import lax
from jax.experimental import pallas as pl
from jax.experimental.pallas import tpu as pltpu
from jax.sharding import PartitionSpec as P

MESH = pl.DeviceIdType.MESH
HALF = 8
MIRRORED = 2
DEPTH = 3


def route(mirrored, sizes, refs, gains_terms, pairs_v, order_v):
    first, groups_j, groups_z, times, vis = sizes
    slots = groups_j * groups_z
    length = slots * times
    tm = lax.axis_index("tm")
    fq = lax.axis_index("freq")
    me_j = tm // groups_z
    me_z = tm % groups_z
    r = SimpleNamespace(**refs)
    if mirrored:
        near, far, me_near, me_far = groups_z, groups_j, me_z, me_j
    else:
        near, far, me_near, me_far = groups_j, groups_z, me_j, me_z
    block = r.x_buf.shape[3]

    def slot(a, b):
        return b * groups_z + a if mirrored else a * groups_z + b

    def dev_near(o):
        return (slot(lax.rem(me_near + o, near), me_far), fq)

    def dev_far(o):
        return (slot(me_near, lax.rem(me_far + o, far)), fq)

    my_times = pl.ds(pl.multiple_of(me_near * times, times), times)
    my_block = pl.ds(pl.multiple_of(me_near * block, block), block)

    def raw_copy(l, o):
        to = lax.rem(me_near + o, near)
        return pltpu.make_async_remote_copy(
            src_ref=vis.at[:, first + l, :, pl.ds(pl.multiple_of(to * block, block), block)],
            dst_ref=r.x_buf.at[l, :, my_times, :],
            send_sem=r.raw_send.at[l, o],
            recv_sem=r.raw_recv.at[l, o],
            device_id=dev_near(o),
            device_id_type=MESH,
        )

    def own_copy(l):
        return pltpu.make_async_copy(
            vis.at[:, first + l, :, my_block], r.x_buf.at[l, :, my_times, :], r.raw_own.at[l]
        )

    def start_raw(l):
        for o in range(1, near):
            raw_copy(l, o).start()
        own_copy(l).start()

    def prepare():
        n_rows = 2 * slots
        n_cols = 2 * near * times
        row_s = lax.broadcasted_iota(jnp.int32, (n_rows, slots), 0)
        chosen = lax.broadcasted_iota(jnp.int32, (n_rows, slots), 1) == slot(row_s % near, row_s // (2 * near))
        mode = jnp.sum(jnp.where(chosen, order_v[...].astype(jnp.float32), 0.0), axis=1, keepdims=True)
        shifted = mode.astype(jnp.int32) - slots // 2
        row = lax.broadcasted_iota(jnp.int32, (n_rows, n_cols), 0)
        col = lax.broadcasted_iota(jnp.int32, (n_rows, n_cols), 1)
        part_out = row // near % 2
        part_in = col // (near * times)
        local = col % (near * times)
        time = slot(local // times, me_far) * times + local % times
        quarter = (part_out - part_in) * (length // 4)
        phase = (shifted * time + quarter) & (length - 1)
        angle = 2.0 * jnp.pi / length * phase.astype(jnp.float32)
        norm = 1.0 / jnp.sqrt(jnp.float32(length))
        r.table_v[...] = (jnp.cos(angle) * norm).astype(jnp.bfloat16)
        feeds = lax.broadcasted_iota(jnp.int32, (gains_terms.shape[1], block), 0)
        picked = []
        for side in range(2):
            picker = (feeds == pairs_v[side : side + 1, my_block]).astype(jnp.float32).astype(jnp.bfloat16)
            found = jnp.dot(gains_terms, picker, preferred_element_type=jnp.float32)
            n = found.shape[0] // 3
            picked.append(found[:n] + found[n : 2 * n] + found[2 * n :])
        chans = picked[0].shape[0] // 2
        gi_re, gi_im = picked[0][:chans], picked[0][chans:]
        gj_re, gj_im = picked[1][:chans], picked[1][chans:]
        r.prod_v[0] = gi_re * gj_re + gi_im * gj_im
        r.prod_v[1] = gi_im * gj_re - gi_re * gj_im

    def part_copy(l, o):
        to = lax.rem(me_far + o, far)
        return pltpu.make_async_remote_copy(
            src_ref=r.part.at[l, to],
            dst_ref=r.gathered.at[l, me_far],
            send_sem=r.part_send.at[l, o],
            recv_sem=r.part_recv.at[l, o],
            device_id=dev_far(o),
            device_id_type=MESH,
        )

    def part_own_copy(l):
        return pltpu.make_async_copy(r.part.at[l, me_far], r.gathered.at[l, me_far], r.part_own.at[l])

    def transform(l):
        own_copy(l).wait()
        for o in range(1, near):
            raw_copy(l, o).wait_recv()
        data = r.x_buf[l].reshape(2 * near * times, block)
        sums = jnp.dot(r.table_v[...], data, preferred_element_type=jnp.float32)
        r.part[l] = sums.astype(jnp.bfloat16).reshape(far, 2 * near, block)
        for o in range(1, far):
            part_copy(l, o).start()
        part_own_copy(l).start()

    def combine(l, rows32, place):
        part_own_copy(l).wait()
        for o in range(1, far):
            part_copy(l, o).wait_recv()
        total = r.gathered[l, 0].astype(jnp.float32)
        for i in range(1, far):
            total = total + r.gathered[l, i].astype(jnp.float32)
        p_re = r.prod_v[0, first + l : first + l + 1, :]
        p_im = r.prod_v[1, first + l : first + l + 1, :]
        t_re, t_im = total[:near], total[near:]
        s_re = t_re * p_re - t_im * p_im
        s_im = t_re * p_im + t_im * p_re
        for i in range(near):
            rows32[i, place : place + 1, :] = s_re[i : i + 1]
            rows32[i, HALF + place : HALF + place + 1, :] = s_im[i : i + 1]

    def drain():
        for l in range(r.x_buf.shape[0]):
            for o in range(1, near):
                raw_copy(l, o).wait_send()
            for o in range(1, far):
                part_copy(l, o).wait_send()

    return SimpleNamespace(
        near=near,
        me_near=me_near,
        first=first,
        block=block,
        dev_near=dev_near,
        start_raw=start_raw,
        prepare=prepare,
        transform=transform,
        combine=combine,
        drain=drain,
        peers=[dev_near(o) for o in range(1, near)],
    )


def unit(way, low, high, kept, beam, basis_v, refs):
    u = SimpleNamespace(**refs)
    rows = slice((way.first + low) * kept, (way.first + high) * kept)

    def loads():
        return [
            pltpu.make_async_copy(
                beam.at[:, rows, i * way.block : (i + 1) * way.block], u.beam_v.at[i], u.load_sem.at[i]
            )
            for i in range(way.near)
        ]

    def spec_copy(o):
        to = lax.rem(way.me_near + o, way.near)
        return pltpu.make_async_remote_copy(
            src_ref=u.spec_out.at[to],
            dst_ref=u.spec_in.at[way.me_near],
            send_sem=u.spec_send.at[o],
            recv_sem=u.spec_recv.at[o],
            device_id=way.dev_near(o),
            device_id_type=MESH,
        )

    own = pltpu.make_async_copy(u.spec_out.at[way.me_near], u.spec_in.at[way.me_near], u.spec_own)

    def send():
        u.spec_out[...] = u.rows32[...].astype(jnp.bfloat16)
        for o in range(1, way.near):
            spec_copy(o).start()
        own.start()

    def finish():
        for copy in loads():
            copy.wait()
        own.wait()
        for o in range(1, way.near):
            spec_copy(o).wait_recv()
        contract = (((1,), (1,)), ((), ()))
        tel = jnp.zeros((u.beam_v.shape[2], 2 * HALF), jnp.float32)
        for i in range(way.near):
            spec = u.spec_in[i]
            wide = spec.astype(jnp.float32)
            turned = jnp.concatenate([-wide[HALF:], wide[:HALF]], axis=0).astype(jnp.bfloat16)
            tel = tel + lax.dot_general(u.beam_v[i, 0], spec, contract, preferred_element_type=jnp.float32)
            tel = tel + lax.dot_general(u.beam_v[i, 1], turned, contract, preferred_element_type=jnp.float32)
        chan_row = lax.broadcasted_iota(jnp.int32, tel.shape, 0) // kept
        chan_col = lax.broadcasted_iota(jnp.int32, tel.shape, 1) % HALF
        tel = jnp.where(chan_row == chan_col, tel, 0.0).astype(jnp.bfloat16)
        return lax.dot_general(
            tel, basis_v[rows, :], (((0,), (0,)), ((), ())), preferred_element_type=jnp.float32
        )

    def clear():
        u.rows32[...] = jnp.zeros(u.rows32.shape, jnp.float32)

    def drain():
        for o in range(1, way.near):
            spec_copy(o).wait_send()

    return SimpleNamespace(loads=loads, send=send, finish=finish, clear=clear, drain=drain, rows32=u.rows32, low=low)


WAY_REFS = ("x_buf", "part", "gathered", "table_v", "prod_v", "raw_send", "raw_recv", "raw_own")
WAY_REFS = WAY_REFS + ("part_send", "part_recv", "part_own")
UNIT_REFS = ("rows32", "spec_out", "spec_in", "beam_v", "spec_send", "spec_recv", "spec_own", "load_sem")


def kernel(dims, vis, gains, pairs, order, beam, basis, out, *scratch):
    groups_j, groups_z, parts_f, chans, times, kept, mirrored = dims
    straight = chans - mirrored
    scratch = list(scratch)

    def take(names):
        return {name: scratch.pop(0) for name in names}

    basis_v, gains_v, pairs_v, order_v, share_out, share_in, share_send, share_recv, small_sem = (
        scratch.pop(0) for _ in range(9)
    )
    tm = lax.axis_index("tm")
    fq = lax.axis_index("freq")
    loads = [
        pltpu.make_async_copy(order, order_v, small_sem.at[0]),
        pltpu.make_async_copy(pairs, pairs_v, small_sem.at[1]),
        pltpu.make_async_copy(gains, gains_v, small_sem.at[2]),
    ]
    basis_load = pltpu.make_async_copy(basis, basis_v, small_sem.at[3])
    for copy in loads:
        copy.start()

    def split_gains():
        whole = gains_v[...]
        high = whole.astype(jnp.bfloat16)
        rest = whole - high.astype(jnp.float32)
        middle = rest.astype(jnp.bfloat16)
        low = (rest - middle.astype(jnp.float32)).astype(jnp.bfloat16)
        return jnp.concatenate([high, middle, low], axis=0)

    way_a_refs = take(WAY_REFS)
    way_b_refs = take(WAY_REFS)
    unit_refs = [take(UNIT_REFS) for _ in range(3)]

    def routes(terms):
        a = route(False, (0, groups_j, groups_z, times, vis), way_a_refs, terms, pairs_v, order_v)
        b = route(True, (straight, groups_j, groups_z, times, vis), way_b_refs, terms, pairs_v, order_v)
        return a, b

    way_a, way_b = routes(None)

    def dev_f(o):
        return (tm, lax.rem(fq + o, parts_f))

    barrier = pltpu.get_barrier_semaphore()
    peers = way_a.peers + way_b.peers + [dev_f(o) for o in range(1, parts_f)]
    for peer in peers:
        pl.semaphore_signal(barrier, inc=1, device_id=peer, device_id_type=MESH)
    pl.semaphore_wait(barrier, len(peers))

    way_a.start_raw(0)
    for l in range(mirrored):
        way_b.start_raw(l)
    for l in range(1, min(DEPTH, straight)):
        way_a.start_raw(l)
    many = unit(way_a, 0, straight - 1, kept, beam, basis_v, unit_refs[0])
    last = unit(way_a, straight - 1, straight, kept, beam, basis_v, unit_refs[1])
    mirror = unit(way_b, 0, mirrored, kept, beam, basis_v, unit_refs[2])
    units = (many, last, mirror)
    basis_load.start()
    for u in units:
        for copy in u.loads():
            copy.start()
    for copy in loads:
        copy.wait()
    for way in routes(split_gains()):
        way.prepare()
    for u in units:
        u.clear()

    def combine_a(l):
        u = many if l < straight - 1 else last
        way_a.combine(l, u.rows32, l - u.low)

    after = {(l + 1) * straight // mirrored - 2: l for l in range(mirrored)}
    pending = []
    for l in range(straight):
        if l + DEPTH < straight:
            way_a.start_raw(l + DEPTH)
        way_a.transform(l)
        if l < straight - 1:
            pending.append(functools.partial(combine_a, l))
        else:
            pending.append(many.send)
        while len(pending) > 1 and l < straight - 1:
            pending.pop(0)()
        if l in after:
            m = after[l]
            way_b.transform(m)
            pending.append(functools.partial(way_b.combine, m, mirror.rows32, m))
    for action in pending:
        action()
    mirror.send()
    combine_a(straight - 1)
    last.send()
    basis_load.wait()
    modes = mirror.finish()
    modes = modes + many.finish()
    modes = modes + last.finish()
    shares = jnp.sum(modes.reshape(2, HALF, modes.shape[1]), axis=1)
    width = modes.shape[1] // parts_f
    share_out[...] = jnp.zeros(share_out.shape, jnp.float32)
    for i in range(parts_f):
        share_out[i, 0:2, :] = shares[:, i * width : (i + 1) * width]

    def share_copy(o):
        to = lax.rem(fq + o, parts_f)
        return pltpu.make_async_remote_copy(
            src_ref=share_out.at[to],
            dst_ref=share_in.at[o],
            send_sem=share_send.at[o],
            recv_sem=share_recv.at[o],
            device_id=dev_f(o),
            device_id_type=MESH,
        )

    for o in range(1, parts_f):
        share_copy(o).start()
    way_a.drain()
    way_b.drain()
    for u in units:
        u.drain()
    total = share_out[fq]
    for o in range(1, parts_f):
        share_copy(o).wait_recv()
        total = total + share_in[o]
    out[...] = total[0:2]
    for o in range(1, parts_f):
        share_copy(o).wait_send()


def on_device(groups_j, mirrored, visibilities, feed_gains, feed_pairs, m_order, beam_rows, kl_basis):
    groups_z = lax.axis_size("tm") // groups_j
    parts_f = lax.axis_size("freq")
    chans, times, baselines = visibilities.shape[1:]
    kept = beam_rows.shape[3]
    modes = kl_basis.shape[3]
    slots = groups_j * groups_z
    dims = (groups_j, groups_z, parts_f, chans, times, kept, mirrored)
    feeds = feed_gains.shape[2]
    width = modes // parts_f
    bf16, f32 = jnp.bfloat16, jnp.float32
    dma = pltpu.SemaphoreType.DMA
    vmem = pltpu.VMEM

    def way_scratch(n, near, far):
        block = baselines // near
        return [
            vmem((n, 2, near * times, block), bf16),
            vmem((n, far, 2 * near, block), bf16),
            vmem((n, far, 2 * near, block), bf16),
            vmem((2 * slots, 2 * near * times), bf16),
            vmem((2, chans, block), f32),
            dma((n, near)),
            dma((n, near)),
            dma((n,)),
            dma((n, far)),
            dma((n, far)),
            dma((n,)),
        ]

    def unit_scratch(n, near):
        block = baselines // near
        return [
            vmem((near, 2 * HALF, block), f32),
            vmem((near, 2 * HALF, block), bf16),
            vmem((near, 2 * HALF, block), bf16),
            vmem((near, 2, n * kept, block), bf16),
            dma((near,)),
            dma((near,)),
            dma,
            dma((near,)),
        ]

    straight = chans - mirrored
    result = pl.pallas_call(
        functools.partial(kernel, dims),
        out_shape=jax.ShapeDtypeStruct((2, width), f32),
        in_specs=[pl.BlockSpec(memory_space=pl.ANY)] * 6,
        out_specs=pl.BlockSpec(memory_space=vmem),
        scratch_shapes=[
            vmem((chans * kept, modes), bf16),
            vmem((2 * chans, feeds), f32),
            vmem((2, baselines), jnp.int32),
            vmem((1, slots), jnp.int32),
            vmem((parts_f, 8, width), f32),
            vmem((parts_f, 8, width), f32),
            dma((parts_f,)),
            dma((parts_f,)),
            dma((4,)),
            *way_scratch(straight, groups_j, groups_z),
            *way_scratch(mirrored, groups_z, groups_j),
            *unit_scratch(straight - 1, groups_j),
            *unit_scratch(1, groups_j),
            *unit_scratch(mirrored, groups_z),
        ],
        compiler_params=pltpu.CompilerParams(
            collective_id=0, has_side_effects=True, vmem_limit_bytes=63 * 2**20
        ),
    )(
        visibilities,
        feed_gains.reshape(2 * chans, feeds),
        feed_pairs.T,
        m_order.reshape(1, slots),
        beam_rows.reshape(2, chans * kept, baselines),
        kl_basis.reshape(chans * kept, modes),
    )
    return result.reshape(2, 1, width)


def solution(mesh, groups_j=8, mirrored=MIRRORED):
    placed = (
        P(None, "freq", "tm", None),
        P(None, "freq", None),
        P(),
        P(),
        P(None, "tm", "freq", None, None),
        P("tm", "freq", None, None),
    )
    return jax.shard_map(
        functools.partial(on_device, groups_j, mirrored),
        mesh=mesh,
        in_specs=placed,
        out_specs=P(None, "tm", "freq"),
        check_vma=False,
    )
```

```python
import functools
from types import SimpleNamespace

import jax
import jax.numpy as jnp
from jax import lax
from jax.experimental import pallas as pl
from jax.experimental.pallas import tpu as pltpu
from jax.sharding import PartitionSpec as P

MESH = pl.DeviceIdType.MESH
HALF = 8
MIRRORED = 2
DEPTH = 3


def route(mirrored, sizes, refs, gains_terms, pairs_v, order_v):
    first, groups_j, groups_z, times, vis = sizes
    slots = groups_j * groups_z
    length = slots * times
    tm = lax.axis_index("tm")
    fq = lax.axis_index("freq")
    me_j = tm // groups_z
    me_z = tm % groups_z
    r = SimpleNamespace(**refs)
    if mirrored:
        near, far, me_near, me_far = groups_z, groups_j, me_z, me_j
    else:
        near, far, me_near, me_far = groups_j, groups_z, me_j, me_z
    block = r.x_buf.shape[3]

    def slot(a, b):
        return b * groups_z + a if mirrored else a * groups_z + b

    def dev_near(o):
        return (slot(lax.rem(me_near + o, near), me_far), fq)

    def dev_far(o):
        return (slot(me_near, lax.rem(me_far + o, far)), fq)

    my_times = pl.ds(pl.multiple_of(me_near * times, times), times)
    my_block = pl.ds(pl.multiple_of(me_near * block, block), block)

    def raw_copy(l, o):
        to = lax.rem(me_near + o, near)
        return pltpu.make_async_remote_copy(
            src_ref=vis.at[:, first + l, :, pl.ds(pl.multiple_of(to * block, block), block)],
            dst_ref=r.x_buf.at[l, :, my_times, :],
            send_sem=r.raw_send.at[l, o],
            recv_sem=r.raw_recv.at[l, o],
            device_id=dev_near(o),
            device_id_type=MESH,
        )

    def own_copy(l):
        return pltpu.make_async_copy(
            vis.at[:, first + l, :, my_block], r.x_buf.at[l, :, my_times, :], r.raw_own.at[l]
        )

    def start_raw(l):
        for o in range(1, near):
            raw_copy(l, o).start()
        own_copy(l).start()

    def prepare():
        n_rows = 2 * slots
        n_cols = 2 * near * times
        row_s = lax.broadcasted_iota(jnp.int32, (n_rows, slots), 0)
        chosen = lax.broadcasted_iota(jnp.int32, (n_rows, slots), 1) == slot(row_s % near, row_s // (2 * near))
        mode = jnp.sum(jnp.where(chosen, order_v[...].astype(jnp.float32), 0.0), axis=1, keepdims=True)
        shifted = mode.astype(jnp.int32) - slots // 2
        row = lax.broadcasted_iota(jnp.int32, (n_rows, n_cols), 0)
        col = lax.broadcasted_iota(jnp.int32, (n_rows, n_cols), 1)
        part_out = row // near % 2
        part_in = col // (near * times)
        local = col % (near * times)
        time = slot(local // times, me_far) * times + local % times
        quarter = (part_out - part_in) * (length // 4)
        phase = (shifted * time + quarter) & (length - 1)
        angle = 2.0 * jnp.pi / length * phase.astype(jnp.float32)
        norm = 1.0 / jnp.sqrt(jnp.float32(length))
        r.table_v[...] = (jnp.cos(angle) * norm).astype(jnp.bfloat16)
        feeds = lax.broadcasted_iota(jnp.int32, (gains_terms.shape[1], block), 0)
        picked = []
        for side in range(2):
            picker = (feeds == pairs_v[side : side + 1, my_block]).astype(jnp.float32).astype(jnp.bfloat16)
            found = jnp.dot(gains_terms, picker, preferred_element_type=jnp.float32)
            n = found.shape[0] // 3
            picked.append(found[:n] + found[n : 2 * n] + found[2 * n :])
        chans = picked[0].shape[0] // 2
        gi_re, gi_im = picked[0][:chans], picked[0][chans:]
        gj_re, gj_im = picked[1][:chans], picked[1][chans:]
        r.prod_v[0] = gi_re * gj_re + gi_im * gj_im
        r.prod_v[1] = gi_im * gj_re - gi_re * gj_im

    def part_copy(l, o):
        to = lax.rem(me_far + o, far)
        return pltpu.make_async_remote_copy(
            src_ref=r.part.at[l, to],
            dst_ref=r.gathered.at[l, me_far],
            send_sem=r.part_send.at[l, o],
            recv_sem=r.part_recv.at[l, o],
            device_id=dev_far(o),
            device_id_type=MESH,
        )

    def part_own_copy(l):
        return pltpu.make_async_copy(r.part.at[l, me_far], r.gathered.at[l, me_far], r.part_own.at[l])

    def transform(l):
        own_copy(l).wait()
        for o in range(1, near):
            raw_copy(l, o).wait_recv()
        data = r.x_buf[l].reshape(2 * near * times, block)
        sums = jnp.dot(r.table_v[...], data, preferred_element_type=jnp.float32)
        r.part[l] = sums.astype(jnp.bfloat16).reshape(far, 2 * near, block)
        for o in range(1, far):
            part_copy(l, o).start()
        part_own_copy(l).start()

    def combine(l, rows32, place):
        part_own_copy(l).wait()
        for o in range(1, far):
            part_copy(l, o).wait_recv()
        total = r.gathered[l, 0].astype(jnp.float32)
        for i in range(1, far):
            total = total + r.gathered[l, i].astype(jnp.float32)
        p_re = r.prod_v[0, first + l : first + l + 1, :]
        p_im = r.prod_v[1, first + l : first + l + 1, :]
        t_re, t_im = total[:near], total[near:]
        s_re = t_re * p_re - t_im * p_im
        s_im = t_re * p_im + t_im * p_re
        for i in range(near):
            rows32[i, place : place + 1, :] = s_re[i : i + 1]
            rows32[i, HALF + place : HALF + place + 1, :] = s_im[i : i + 1]

    def drain():
        for l in range(r.x_buf.shape[0]):
            for o in range(1, near):
                raw_copy(l, o).wait_send()
            for o in range(1, far):
                part_copy(l, o).wait_send()

    return SimpleNamespace(
        near=near,
        me_near=me_near,
        first=first,
        block=block,
        dev_near=dev_near,
        start_raw=start_raw,
        prepare=prepare,
        transform=transform,
        combine=combine,
        drain=drain,
        peers=[dev_near(o) for o in range(1, near)],
    )


def unit(way, low, high, kept, beam, basis_v, refs):
    u = SimpleNamespace(**refs)
    rows = slice((way.first + low) * kept, (way.first + high) * kept)

    def loads():
        return [
            pltpu.make_async_copy(
                beam.at[:, rows, i * way.block : (i + 1) * way.block], u.beam_v.at[i], u.load_sem.at[i]
            )
            for i in range(way.near)
        ]

    def spec_copy(o):
        to = lax.rem(way.me_near + o, way.near)
        return pltpu.make_async_remote_copy(
            src_ref=u.spec_out.at[to],
            dst_ref=u.spec_in.at[way.me_near],
            send_sem=u.spec_send.at[o],
            recv_sem=u.spec_recv.at[o],
            device_id=way.dev_near(o),
            device_id_type=MESH,
        )

    own = pltpu.make_async_copy(u.spec_out.at[way.me_near], u.spec_in.at[way.me_near], u.spec_own)

    def send():
        u.spec_out[...] = u.rows32[...].astype(jnp.bfloat16)
        for o in range(1, way.near):
            spec_copy(o).start()
        own.start()

    def finish():
        for copy in loads():
            copy.wait()
        own.wait()
        for o in range(1, way.near):
            spec_copy(o).wait_recv()
        contract = (((1,), (1,)), ((), ()))
        tel = jnp.zeros((u.beam_v.shape[2], 2 * HALF), jnp.float32)
        for i in range(way.near):
            spec = u.spec_in[i]
            wide = spec.astype(jnp.float32)
            turned = jnp.concatenate([-wide[HALF:], wide[:HALF]], axis=0).astype(jnp.bfloat16)
            tel = tel + lax.dot_general(u.beam_v[i, 0], spec, contract, preferred_element_type=jnp.float32)
            tel = tel + lax.dot_general(u.beam_v[i, 1], turned, contract, preferred_element_type=jnp.float32)
        chan_row = lax.broadcasted_iota(jnp.int32, tel.shape, 0) // kept
        chan_col = lax.broadcasted_iota(jnp.int32, tel.shape, 1) % HALF
        tel = jnp.where(chan_row == chan_col, tel, 0.0).astype(jnp.bfloat16)
        return lax.dot_general(
            tel, basis_v[rows, :], (((0,), (0,)), ((), ())), preferred_element_type=jnp.float32
        )

    def clear():
        u.rows32[...] = jnp.zeros(u.rows32.shape, jnp.float32)

    def drain():
        for o in range(1, way.near):
            spec_copy(o).wait_send()

    return SimpleNamespace(loads=loads, send=send, finish=finish, clear=clear, drain=drain, rows32=u.rows32, low=low)


WAY_REFS = ("x_buf", "part", "gathered", "table_v", "prod_v", "raw_send", "raw_recv", "raw_own")
WAY_REFS = WAY_REFS + ("part_send", "part_recv", "part_own")
UNIT_REFS = ("rows32", "spec_out", "spec_in", "beam_v", "spec_send", "spec_recv", "spec_own", "load_sem")


def kernel(dims, vis, gains, pairs, order, beam, basis, out, *scratch):
    groups_j, groups_z, parts_f, chans, times, kept, mirrored = dims
    straight = chans - mirrored
    scratch = list(scratch)

    def take(names):
        return {name: scratch.pop(0) for name in names}

    basis_v, gains_v, pairs_v, order_v, share_out, share_in, share_send, share_recv, small_sem = (
        scratch.pop(0) for _ in range(9)
    )
    tm = lax.axis_index("tm")
    fq = lax.axis_index("freq")
    loads = [
        pltpu.make_async_copy(order, order_v, small_sem.at[0]),
        pltpu.make_async_copy(pairs, pairs_v, small_sem.at[1]),
        pltpu.make_async_copy(gains, gains_v, small_sem.at[2]),
    ]
    basis_load = pltpu.make_async_copy(basis, basis_v, small_sem.at[3])
    for copy in loads:
        copy.start()

    def split_gains():
        whole = gains_v[...]
        high = whole.astype(jnp.bfloat16)
        rest = whole - high.astype(jnp.float32)
        middle = rest.astype(jnp.bfloat16)
        low = (rest - middle.astype(jnp.float32)).astype(jnp.bfloat16)
        return jnp.concatenate([high, middle, low], axis=0)

    way_a_refs = take(WAY_REFS)
    way_b_refs = take(WAY_REFS)
    unit_refs = [take(UNIT_REFS) for _ in range(3)]

    def routes(terms):
        a = route(False, (0, groups_j, groups_z, times, vis), way_a_refs, terms, pairs_v, order_v)
        b = route(True, (straight, groups_j, groups_z, times, vis), way_b_refs, terms, pairs_v, order_v)
        return a, b

    way_a, way_b = routes(None)

    def dev_f(o):
        return (tm, lax.rem(fq + o, parts_f))

    barrier = pltpu.get_barrier_semaphore()
    peers = way_a.peers + way_b.peers + [dev_f(o) for o in range(1, parts_f)]
    for peer in peers:
        pl.semaphore_signal(barrier, inc=1, device_id=peer, device_id_type=MESH)
    pl.semaphore_wait(barrier, len(peers))

    way_a.start_raw(0)
    for l in range(mirrored):
        way_b.start_raw(l)
    for l in range(1, min(DEPTH, straight)):
        way_a.start_raw(l)
    many = unit(way_a, 0, straight - 1, kept, beam, basis_v, unit_refs[0])
    last = unit(way_a, straight - 1, straight, kept, beam, basis_v, unit_refs[1])
    mirror = unit(way_b, 0, mirrored, kept, beam, basis_v, unit_refs[2])
    units = (many, last, mirror)
    basis_load.start()
    for u in units:
        for copy in u.loads():
            copy.start()
    for copy in loads:
        copy.wait()
    for way in routes(split_gains()):
        way.prepare()
    for u in units:
        u.clear()

    def combine_a(l):
        u = many if l < straight - 1 else last
        way_a.combine(l, u.rows32, l - u.low)

    after = {(l + 1) * straight // mirrored - 2: l for l in range(mirrored)}
    pending = []
    for l in range(straight):
        if l + DEPTH < straight:
            way_a.start_raw(l + DEPTH)
        way_a.transform(l)
        if l < straight - 1:
            pending.append(functools.partial(combine_a, l))
        else:
            pending.append(many.send)
        while len(pending) > 3 and l < straight - 1:
            pending.pop(0)()
        if l in after:
            m = after[l]
            way_b.transform(m)
            pending.append(functools.partial(way_b.combine, m, mirror.rows32, m))
    for action in pending:
        action()
    mirror.send()
    combine_a(straight - 1)
    last.send()
    basis_load.wait()
    modes = mirror.finish()
    modes = modes + many.finish()
    modes = modes + last.finish()
    shares = jnp.sum(modes.reshape(2, HALF, modes.shape[1]), axis=1)
    width = modes.shape[1] // parts_f
    share_out[...] = jnp.zeros(share_out.shape, jnp.float32)
    for i in range(parts_f):
        share_out[i, 0:2, :] = shares[:, i * width : (i + 1) * width]

    def share_copy(o):
        to = lax.rem(fq + o, parts_f)
        return pltpu.make_async_remote_copy(
            src_ref=share_out.at[to],
            dst_ref=share_in.at[o],
            send_sem=share_send.at[o],
            recv_sem=share_recv.at[o],
            device_id=dev_f(o),
            device_id_type=MESH,
        )

    for o in range(1, parts_f):
        share_copy(o).start()
    way_a.drain()
    way_b.drain()
    for u in units:
        u.drain()
    total = share_out[fq]
    for o in range(1, parts_f):
        share_copy(o).wait_recv()
        total = total + share_in[o]
    out[...] = total[0:2]
    for o in range(1, parts_f):
        share_copy(o).wait_send()


def on_device(groups_j, mirrored, visibilities, feed_gains, feed_pairs, m_order, beam_rows, kl_basis):
    groups_z = lax.axis_size("tm") // groups_j
    parts_f = lax.axis_size("freq")
    chans, times, baselines = visibilities.shape[1:]
    kept = beam_rows.shape[3]
    modes = kl_basis.shape[3]
    slots = groups_j * groups_z
    dims = (groups_j, groups_z, parts_f, chans, times, kept, mirrored)
    feeds = feed_gains.shape[2]
    width = modes // parts_f
    bf16, f32 = jnp.bfloat16, jnp.float32
    dma = pltpu.SemaphoreType.DMA
    vmem = pltpu.VMEM

    def way_scratch(n, near, far):
        block = baselines // near
        return [
            vmem((n, 2, near * times, block), bf16),
            vmem((n, far, 2 * near, block), bf16),
            vmem((n, far, 2 * near, block), bf16),
            vmem((2 * slots, 2 * near * times), bf16),
            vmem((2, chans, block), f32),
            dma((n, near)),
            dma((n, near)),
            dma((n,)),
            dma((n, far)),
            dma((n, far)),
            dma((n,)),
        ]

    def unit_scratch(n, near):
        block = baselines // near
        return [
            vmem((near, 2 * HALF, block), f32),
            vmem((near, 2 * HALF, block), bf16),
            vmem((near, 2 * HALF, block), bf16),
            vmem((near, 2, n * kept, block), bf16),
            dma((near,)),
            dma((near,)),
            dma,
            dma((near,)),
        ]

    straight = chans - mirrored
    result = pl.pallas_call(
        functools.partial(kernel, dims),
        out_shape=jax.ShapeDtypeStruct((2, width), f32),
        in_specs=[pl.BlockSpec(memory_space=pl.ANY)] * 6,
        out_specs=pl.BlockSpec(memory_space=vmem),
        scratch_shapes=[
            vmem((chans * kept, modes), bf16),
            vmem((2 * chans, feeds), f32),
            vmem((2, baselines), jnp.int32),
            vmem((1, slots), jnp.int32),
            vmem((parts_f, 8, width), f32),
            vmem((parts_f, 8, width), f32),
            dma((parts_f,)),
            dma((parts_f,)),
            dma((4,)),
            *way_scratch(straight, groups_j, groups_z),
            *way_scratch(mirrored, groups_z, groups_j),
            *unit_scratch(straight - 1, groups_j),
            *unit_scratch(1, groups_j),
            *unit_scratch(mirrored, groups_z),
        ],
        compiler_params=pltpu.CompilerParams(
            collective_id=0, has_side_effects=True, vmem_limit_bytes=63 * 2**20
        ),
    )(
        visibilities,
        feed_gains.reshape(2 * chans, feeds),
        feed_pairs.T,
        m_order.reshape(1, slots),
        beam_rows.reshape(2, chans * kept, baselines),
        kl_basis.reshape(chans * kept, modes),
    )
    return result.reshape(2, 1, width)


def solution(mesh, groups_j=8, mirrored=MIRRORED):
    placed = (
        P(None, "freq", "tm", None),
        P(None, "freq", None),
        P(),
        P(),
        P(None, "tm", "freq", None, None),
        P("tm", "freq", None, None),
    )
    return jax.shard_map(
        functools.partial(on_device, groups_j, mirrored),
        mesh=mesh,
        in_specs=placed,
        out_specs=P(None, "tm", "freq"),
        check_vma=False,
    )
```
